32 devices in a mesh: groups: 2 (over x), hid: 16 (over z, y, core).
Axes of the slice: x: 2, y: 2, z: 4, core: 2. Of those that a mesh axis runs over, the one named last changes fastest.
Arguments:
- tokens: bfloat16 [256, 8192], P(('groups', 'hid')), parts along dimension 0, may hold values from -6 to 6
- norm_gain: float32 [8192], replicated, may hold values from 0.1 to 1.9
- gate_weight: bfloat16 [8192, 16384], P(None, 'hid'), may hold values from -0.0625 to 0.0625
- up_weight: bfloat16 [8192, 16384], P(None, 'hid'), may hold values from -0.0625 to 0.0625
- down_weight: bfloat16 [16384, 8192], P('hid'), may hold values from -0.046875 to 0.046875
- clip_scale: float32 [16384], P('hid'), may hold values from 0.002 to 0.02
Outputs:
- mixed: bfloat16 [256, 8192], P(('groups', 'hid')), parts along dimension 0
The draws below stay inside these ranges and needn't reach their ends.
There are 2 independent parts, one for each index of `groups`. The reference program is written for one: setup_inputs(seed, part) draws one part's arguments, and reference() takes and returns one part's arrays. A program takes and returns all parts, laid end to end along the dimension named above; an argument that names none is the same for every part. Nothing has to cross between parts.
All inputs are finite; a program needn't handle non-finite values.
Results may differ from the reference program's by a relative error of at most 0.006.
Values may be sent and summed in bfloat16 or wider, within the bound.
A program may use at most 128 MiB of HBM per device.

```python
import math
import jax
import jax.numpy as jnp
from jax import lax

D = 8192
FF = 16384
BLOCK = 256
TOKENS = 128


def block_scale(own_key, extent, split, smallest, top_value):
    level = 1.0
    for axis_at, blocks in split:
        draws = jax.random.uniform(jax.random.fold_in(jax.random.fold_in(own_key, 6), axis_at), (blocks,), jnp.float32, smallest / len(split), top_value / len(split))
        level = level * jnp.repeat(jnp.exp(draws), extent[axis_at] // blocks).reshape((-1,) + (1,) * (len(extent) - 1 - axis_at))
    return level


def scatter_about(rng, shape, width, reach, split=(), kind=jnp.bfloat16):
    array = jax.random.normal(rng, shape, jnp.float32) * width
    if len(split) > 0:
        array = block_scale(rng, shape, split, -0.22, 0.18) * array
    return jnp.clip(array, min=-reach, max=reach).astype(kind)


def setup_inputs(seed: int = 0, part: int = 0) -> dict:
    streams_of = jax.random.split(jax.random.key(seed), 7)
    part_splits = jax.random.split(jax.random.fold_in(streams_of[6], part), 7)
    tokens = scatter_about(part_splits[0], (TOKENS, D), 1.0, 6.0, ((0, 16),))
    norm_gain = jnp.clip(1.0 + 0.18 * jax.random.normal(streams_of[1], (D,), jnp.float32), 0.1, 1.9)
    gate_weight = scatter_about(streams_of[2], (D, FF), D ** -0.5, 0.0625, ((1, 16),))
    up_weight = scatter_about(streams_of[3], (D, FF), D ** -0.5, 0.0625, ((1, 16),))
    down_weight = scatter_about(streams_of[4], (FF, D), FF ** -0.5, 0.046875, ((0, 16),))
    clip_scale = jnp.clip(jnp.exp(math.log(0.02) - 2.30258502 * jax.random.uniform(streams_of[5], (FF,), jnp.float32) ** block_scale(streams_of[5], (FF,), ((0, 16),), -0.2, 0.2)), 0.002, 0.02)
    return dict(tokens=tokens, norm_gain=norm_gain, gate_weight=gate_weight, up_weight=up_weight, down_weight=down_weight, clip_scale=clip_scale)


def hadamard(count):
    rows = jnp.arange(count, dtype=jnp.int32)[:, None]
    cols = jnp.arange(count, dtype=jnp.int32)[None, :]
    both = rows & cols
    parity = jnp.zeros((count, count), jnp.int32)
    for place in range(max(count.bit_length(), 1)):
        parity = parity + (both >> place & 1)
    return jnp.where(parity % 2 == 0, 1.0, -1.0).astype(jnp.float32)

def reference(tokens, norm_gain, gate_weight, up_weight, down_weight, clip_scale):
    values = tokens.astype(jnp.float32)
    inverse = lax.rsqrt(lax.optimization_barrier(jnp.mean(values * values, axis=-1, keepdims=True)) + 1e-05)
    normed = (values * inverse * norm_gain).astype(jnp.bfloat16)
    gate = jnp.dot(normed, gate_weight, preferred_element_type=jnp.float32)
    up = jnp.dot(normed, up_weight, preferred_element_type=jnp.float32)
    hidden = jax.nn.silu(gate) * up
    blocks = FF // BLOCK
    shaped = hidden.reshape(TOKENS, blocks, BLOCK)
    shaped = jnp.einsum('tbc,cd->tbd', shaped, hadamard(BLOCK), precision=lax.Precision.HIGHEST)
    shaped = jnp.einsum('tbc,be->tec', shaped, hadamard(blocks), precision=lax.Precision.HIGHEST)
    rotated = shaped.reshape(TOKENS, FF) / jnp.sqrt(jnp.float32(FF))
    limit = 127.0 * clip_scale
    clipped = jnp.clip(rotated, -limit, limit).astype(jnp.bfloat16)
    result = values + jnp.dot(clipped, down_weight, preferred_element_type=jnp.float32)
    return result.astype(jnp.bfloat16)
```

```python
import functools
import math

import jax
import jax.numpy as jnp
from jax import lax
from jax.experimental import pallas as pl
from jax.experimental.pallas import tpu as pltpu
from jax.sharding import PartitionSpec as P

BLOCK = 256
STEPS = 4
TILE = 256
MESH = pl.DeviceIdType.MESH
BF = jnp.bfloat16
F32 = jnp.float32


def walsh(parts):
    parts = list(parts)
    half = 1
    while half < len(parts):
        for at in range(len(parts)):
            if at & half == 0:
                low, high = parts[at], parts[at + half]
                parts[at], parts[at + half] = low + high, low - high
        half *= 2
    return parts


def kernel(n, tok, gain, wg, wu, wd, clip, out,
           pair, x, vg, vu, vd, gate, up, table, hs, hr, bs, br, y,
           cs, cr, own, ys, yr, zs, zr, fs, fr, fk,
           wsem, dsem, pair_sem, ag_send, z_recv, y_recv, c_recv,
           a_send, a_recv, rs_send, rc_recv, ry_recv, rz_recv, rf_recv):
    me = lax.axis_index("hid")
    line = n // 4
    a, b, c = me // 4, (me // 2) % 2, me % 2
    rows, width = tok.shape
    both = 2 * rows
    local = vg.shape[1]
    total = n * rows
    span = width // STEPS
    piece = span // 2
    outs = out.shape[1]
    ospan = outs // STEPS
    opiece = ospan // 2
    core_peer = me + 1 - 2 * c
    y_peer = (a * 2 + 1 - b) * 2 + c

    def at_line(shift):
        return lax.rem(a + shift, line)

    def device(a_at):
        return (a_at * 2 + b) * 2 + c

    def strip(a_at, b_at):
        return pl.ds(pl.multiple_of((a_at * 2 + b_at) * both, both), both)

    def send(src, dst, ssem, rsem, to):
        pltpu.make_async_remote_copy(
            src_ref=src, dst_ref=dst, send_sem=ssem, recv_sem=rsem,
            device_id={"hid": to}, device_id_type=MESH).start()

    def settle(ref, sem):
        pltpu.make_async_copy(ref, ref, sem).wait()

    weight_copies = []
    for s in range(STEPS):
        part = pl.ds(s * span, span)
        weight_copies.append((
            pltpu.make_async_copy(wg.at[part, :], vg.at[part, :], wsem.at[0, s]),
            pltpu.make_async_copy(wu.at[part, :], vu.at[part, :], wsem.at[1, s])))
        for copy in weight_copies[-1]:
            copy.start()
    down_copies = []
    for t in range(STEPS):
        part = pl.ds(t * ospan, ospan)
        down_copies.append(pltpu.make_async_copy(wd.at[:, part], vd.at[:, part], dsem.at[t]))
        down_copies[-1].start()

    barrier = pltpu.get_barrier_semaphore()
    for shift in range(1, n):
        pl.semaphore_signal(barrier, inc=1, device_id={"hid": lax.rem(me + shift, n)}, device_id_type=MESH)
    pl.semaphore_wait(barrier, n - 1)

    send(tok, pair, pair_sem.at[0], pair_sem.at[1], core_peer)
    at_row = lax.broadcasted_iota(jnp.int32, (BLOCK, BLOCK), 0)
    at_col = lax.broadcasted_iota(jnp.int32, (BLOCK, BLOCK), 1)
    bits = at_row & at_col
    folded = bits
    for place in range(1, (BLOCK - 1).bit_length()):
        folded = folded ^ (bits >> place)
    table[...] = (1 - 2 * (folded & 1)).astype(F32).astype(BF)

    def normalized(ref):
        values = ref[...].astype(F32)
        inverse = lax.rsqrt(jnp.mean(values * values, axis=-1, keepdims=True) + 1e-05)
        return values * inverse * gain[...]

    mine = normalized(tok)
    settle(pair, pair_sem.at[1])
    other = normalized(pair)
    first = c == 0
    x[strip(a, b), :] = jnp.concatenate(
        [jnp.where(first, mine, other), jnp.where(first, other, mine)], axis=0).astype(BF)

    def cols(s, half):
        return pl.ds(pl.multiple_of(s * span + half * piece, piece), piece)

    for s in range(STEPS):
        block = x.at[strip(a, b), cols(s, c)]
        send(block, block, ag_send, y_recv.at[s, 0], y_peer)
        for shift in range(1, line):
            send(block, block, ag_send, z_recv.at[s, shift], device(at_line(shift)))

    def relay(s):
        for shift in range(1, line):
            block = x.at[strip(at_line(line - shift), b), cols(s, c)]
            settle(block, z_recv.at[s, shift])
            send(block, block, ag_send, y_recv.at[s, shift], y_peer)
            send(block, block, ag_send, c_recv.at[s], core_peer)
        for shift in range(line):
            block = x.at[strip(at_line(line - shift), 1 - b), cols(s, c)]
            settle(block, y_recv.at[s, shift])
            send(block, block, ag_send, c_recv.at[s], core_peer)

    def project(s):
        settle(x.at[pl.ds(0, total - both), cols(s, 1 - c)], c_recv.at[s])
        for copy in weight_copies[s]:
            copy.wait()
        part = pl.ds(s * span, span)

        @pl.loop(0, local // TILE)
        def _(j):
            tile = pl.ds(pl.multiple_of(j * TILE, TILE), TILE)
            for acc, weight in ((gate, vg), (up, vu)):
                term = jnp.dot(x[:, part], weight[part, tile], preferred_element_type=F32)
                acc[:, tile] = term if s == 0 else acc[:, tile] + term

    relay(0)
    for s in range(STEPS):
        if s + 1 < STEPS:
            relay(s + 1)
        project(s)

    blocks = []
    for at in range(local // BLOCK):
        tile = pl.ds(at * BLOCK, BLOCK)
        value = gate[:, tile]
        hidden = value / (1.0 + jnp.exp(-value)) * up[:, tile]
        gate[:, tile] = jnp.dot(hidden.astype(BF), table[...], preferred_element_type=F32)
    half = local // 2
    for d in range(n):
        part = pl.ds(d * rows, rows)
        values = gate[part, :]
        turned = walsh([values[:, at * BLOCK:(at + 1) * BLOCK] for at in range(local // BLOCK)])
        values = turned[0] if len(turned) == 1 else jnp.concatenate(turned, axis=1)
        hs[d] = jnp.concatenate([values[:, :half], values[:, half:]], axis=0).astype(BF)

    def exchange(src, dst, at):
        for shift in range(1, n):
            to = lax.rem(me + shift, n)
            send(src.at[to], dst.at[me], a_send.at[at], a_recv.at[at], to)
        dst[me] = src[me]
        settle(dst.at[pl.ds(0, n - 1)], a_recv.at[at])

    exchange(hs, hr, 0)
    factor = 1.0 / math.sqrt(n * local)
    lanes = 128
    for j in range(half // lanes):
        tile = pl.ds(j * lanes, lanes)
        turned = walsh([hr[d, :, tile].astype(F32) for d in range(n)])
        for d in range(n):
            bs[d, :, tile] = (turned[d] * factor).astype(BF)
    exchange(bs, br, 1)

    limit = 127.0 * clip[...]
    for q in range(n // 2):
        pieces = []
        for d in (2 * q, 2 * q + 1):
            values = br[d].astype(F32)
            pieces.append(jnp.concatenate([values[:rows], values[rows:]], axis=1))
        values = jnp.concatenate(pieces, axis=0)
        y[pl.ds(q * both, both), :] = jnp.clip(values, -limit, limit).astype(BF)

    def product(t, half_at, j):
        tile = pl.ds(pl.multiple_of(t * ospan + half_at * opiece + j * TILE, TILE), TILE)
        return jnp.dot(y[...], vd[:, tile], preferred_element_type=F32)

    def down(t):
        down_copies[t].wait()

        @pl.loop(0, opiece // TILE)
        def _(j):
            cs[t, :, pl.ds(pl.multiple_of(j * TILE, TILE), TILE)] = product(t, 1 - c, j).astype(BF)

        send(cs.at[t], cr.at[t], rs_send.at[0], rc_recv.at[t], core_peer)

        @pl.loop(0, opiece // TILE)
        def _(j):
            own[t, :, pl.ds(pl.multiple_of(j * TILE, TILE), TILE)] = product(t, c, j)

    def over_rows(t):
        settle(cr.at[t], rc_recv.at[t])
        for to in range(line):
            part = strip(to, 1 - b)
            ys[t, pl.ds(to * both, both), :] = (own[t, part, :] + cr[t, part, :].astype(F32)).astype(BF)
        send(ys.at[t], yr.at[t], rs_send.at[1], ry_recv.at[t], y_peer)

    def column_sum(t, a_at):
        part = strip(a_at, b)
        landed = yr[t, pl.ds(pl.multiple_of(a_at * both, both), both), :]
        return own[t, part, :] + cr[t, part, :].astype(F32) + landed.astype(F32)

    def over_line(t):
        settle(yr.at[t], ry_recv.at[t])
        for shift in range(1, line):
            zs[t, shift] = column_sum(t, at_line(shift)).astype(BF)
        for shift in range(1, line):
            send(zs.at[t, shift], zr.at[t, shift], rs_send.at[2], rz_recv.at[t], device(at_line(shift)))

    def finish(t):
        settle(zr.at[t, pl.ds(1, line - 1)], rz_recv.at[t])
        values = column_sum(t, a)
        for shift in range(1, line):
            values = values + zr[t, shift].astype(F32)
        fs[t] = jnp.where(first, values[rows:], values[:rows])
        fk[t] = jnp.where(first, values[:rows], values[rows:])
        send(fs.at[t], fr.at[t], rs_send.at[3], rf_recv.at[t], core_peer)

    for t in range(STEPS + 3):
        if t < STEPS:
            down(t)
        if 0 <= t - 1 < STEPS:
            over_rows(t - 1)
        if 0 <= t - 2 < STEPS:
            over_line(t - 2)
        if 0 <= t - 3 < STEPS:
            finish(t - 3)
    for t in range(STEPS):
        settle(fr.at[t], rf_recv.at[t])
        for half_at, sums in ((c, fk), (1 - c, fr)):
            part = pl.ds(pl.multiple_of(t * ospan + half_at * opiece, opiece), opiece)
            out[:, part] = (tok[:, part].astype(F32) + sums[t]).astype(out.dtype)

    settle(tok, pair_sem.at[0])
    settle(x.at[pl.ds(0, total - both), :], ag_send)
    settle(hs.at[pl.ds(0, n - 1)], a_send.at[0])
    settle(bs.at[pl.ds(0, n - 1)], a_send.at[1])
    settle(cs, rs_send.at[0])
    settle(ys, rs_send.at[1])
    settle(zs.at[:, pl.ds(1, line - 1)], rs_send.at[2])
    settle(fs, rs_send.at[3])


def layer(n, tokens, norm_gain, gate_weight, up_weight, down_weight, clip_scale):
    rows, width = tokens.shape
    local = gate_weight.shape[1]
    outs = down_weight.shape[1]
    total, both, line = n * rows, 2 * rows, n // 4
    opiece = outs // STEPS // 2
    vmem = pl.BlockSpec(memory_space=pltpu.VMEM)
    hbm = pl.BlockSpec(memory_space=pl.ANY)
    dma = pltpu.SemaphoreType.DMA
    swap = pltpu.VMEM((n, both, local // 2), BF)
    return pl.pallas_call(
        functools.partial(kernel, n),
        out_shape=jax.ShapeDtypeStruct((rows, outs), BF),
        in_specs=[vmem, vmem, hbm, hbm, hbm, vmem],
        out_specs=vmem,
        scratch_shapes=[
            pltpu.VMEM((rows, width), BF),
            pltpu.VMEM((total, width), BF),
            pltpu.VMEM((width, local), BF),
            pltpu.VMEM((width, local), BF),
            pltpu.VMEM((local, outs), BF),
            pltpu.VMEM((total, local), F32),
            pltpu.VMEM((total, local), F32),
            pltpu.VMEM((BLOCK, BLOCK), BF),
            swap, swap, swap, swap,
            pltpu.VMEM((total, local), BF),
            pltpu.VMEM((STEPS, total, opiece), BF),
            pltpu.VMEM((STEPS, total, opiece), BF),
            pltpu.VMEM((STEPS, total, opiece), F32),
            pltpu.VMEM((STEPS, line * both, opiece), BF),
            pltpu.VMEM((STEPS, line * both, opiece), BF),
            pltpu.VMEM((STEPS, line, both, opiece), BF),
            pltpu.VMEM((STEPS, line, both, opiece), BF),
            pltpu.VMEM((STEPS, rows, opiece), F32),
            pltpu.VMEM((STEPS, rows, opiece), F32),
            pltpu.VMEM((STEPS, rows, opiece), F32),
            dma((2, STEPS)), dma((STEPS,)), dma((2,)), dma(()),
            dma((STEPS, line)), dma((STEPS, line)), dma((STEPS,)),
            dma((2,)), dma((2,)), dma((4,)),
            dma((STEPS,)), dma((STEPS,)), dma((STEPS,)), dma((STEPS,)),
        ],
        compiler_params=pltpu.CompilerParams(
            collective_id=0, has_side_effects=True, vmem_limit_bytes=67043328),
    )(tokens, norm_gain.reshape(1, -1), gate_weight, up_weight, down_weight, clip_scale.reshape(1, -1))


def solution(mesh):
    in_specs = (
        P(("groups", "hid"), None),
        P(),
        P(None, "hid"),
        P(None, "hid"),
        P("hid", None),
        P("hid"),
    )
    return jax.shard_map(
        functools.partial(layer, mesh.shape["hid"]), mesh=mesh, in_specs=in_specs,
        out_specs=P(("groups", "hid"), None), check_vma=False)
```

```python
import functools
import math

import jax
import jax.numpy as jnp
from jax import lax
from jax.experimental import pallas as pl
from jax.experimental.pallas import tpu as pltpu
from jax.sharding import PartitionSpec as P

BLOCK = 256
STEPS = 4
OUT_STEPS = 8
LAG = (1, 4, 7)
TILE = 256
MESH = pl.DeviceIdType.MESH
BF = jnp.bfloat16
F32 = jnp.float32


def walsh(parts):
    parts = list(parts)
    half = 1
    while half < len(parts):
        for at in range(len(parts)):
            if at & half == 0:
                low, high = parts[at], parts[at + half]
                parts[at], parts[at + half] = low + high, low - high
        half *= 2
    return parts


def kernel(n, tok, gain, wg, wu, wd, clip, out,
           pair, x, vg, vu, vd, gate, up, table, hs, hr, bs, br, y,
           cs, cr, own, ys, yr, zs, zr, fs, fr, fk,
           wsem, dsem, pair_sem, ag_send, z_recv, y_recv, c_recv,
           a_send, a_recv, rs_send, rc_recv, ry_recv, rz_recv, rf_recv):
    me = lax.axis_index("hid")
    line = n // 4
    a, b, c = me // 4, (me // 2) % 2, me % 2
    rows, width = tok.shape
    both = 2 * rows
    local = vg.shape[1]
    total = n * rows
    span = width // STEPS
    piece = span // 2
    outs = out.shape[1]
    ospan = outs // OUT_STEPS
    opiece = ospan // 2
    core_peer = me + 1 - 2 * c
    y_peer = (a * 2 + 1 - b) * 2 + c

    def at_line(shift):
        return lax.rem(a + shift, line)

    def device(a_at):
        return (a_at * 2 + b) * 2 + c

    def strip(a_at, b_at):
        return pl.ds(pl.multiple_of((a_at * 2 + b_at) * both, both), both)

    def send(src, dst, ssem, rsem, to):
        pltpu.make_async_remote_copy(
            src_ref=src, dst_ref=dst, send_sem=ssem, recv_sem=rsem,
            device_id={"hid": to}, device_id_type=MESH).start()

    def settle(ref, sem):
        pltpu.make_async_copy(ref, ref, sem).wait()

    weight_copies = []
    for s in range(STEPS):
        part = pl.ds(s * span, span)
        weight_copies.append((
            pltpu.make_async_copy(wg.at[part, :], vg.at[part, :], wsem.at[0, s]),
            pltpu.make_async_copy(wu.at[part, :], vu.at[part, :], wsem.at[1, s])))
        for copy in weight_copies[-1]:
            copy.start()
    down_copies = []
    for t in range(OUT_STEPS):
        part = pl.ds(t * ospan, ospan)
        down_copies.append(pltpu.make_async_copy(wd.at[:, part], vd.at[:, part], dsem.at[t]))
        down_copies[-1].start()

    barrier = pltpu.get_barrier_semaphore()
    for shift in range(1, n):
        pl.semaphore_signal(barrier, inc=1, device_id={"hid": lax.rem(me + shift, n)}, device_id_type=MESH)
    pl.semaphore_wait(barrier, n - 1)

    send(tok, pair, pair_sem.at[0], pair_sem.at[1], core_peer)
    at_row = lax.broadcasted_iota(jnp.int32, (BLOCK, BLOCK), 0)
    at_col = lax.broadcasted_iota(jnp.int32, (BLOCK, BLOCK), 1)
    bits = at_row & at_col
    folded = bits
    for place in range(1, (BLOCK - 1).bit_length()):
        folded = folded ^ (bits >> place)
    table[...] = (1 - 2 * (folded & 1)).astype(F32).astype(BF)

    def normalized(ref):
        values = ref[...].astype(F32)
        inverse = lax.rsqrt(jnp.mean(values * values, axis=-1, keepdims=True) + 1e-05)
        return values * inverse * gain[...]

    mine = normalized(tok)
    settle(pair, pair_sem.at[1])
    other = normalized(pair)
    first = c == 0
    x[strip(a, b), :] = jnp.concatenate(
        [jnp.where(first, mine, other), jnp.where(first, other, mine)], axis=0).astype(BF)

    def cols(s, half):
        return pl.ds(pl.multiple_of(s * span + half * piece, piece), piece)

    for s in range(STEPS):
        block = x.at[strip(a, b), cols(s, c)]
        send(block, block, ag_send, y_recv.at[s, 0], y_peer)
        for shift in range(1, line):
            send(block, block, ag_send, z_recv.at[s, shift], device(at_line(shift)))

    def relay_over(s):
        for shift in range(1, line):
            block = x.at[strip(at_line(line - shift), b), cols(s, c)]
            settle(block, z_recv.at[s, shift])
            send(block, block, ag_send, y_recv.at[s, shift], y_peer)
            send(block, block, ag_send, c_recv.at[s], core_peer)

    def relay_core(s):
        for shift in range(line):
            block = x.at[strip(at_line(line - shift), 1 - b), cols(s, c)]
            settle(block, y_recv.at[s, shift])
            send(block, block, ag_send, c_recv.at[s], core_peer)

    def project(s):
        settle(x.at[pl.ds(0, total - both), cols(s, 1 - c)], c_recv.at[s])
        for copy in weight_copies[s]:
            copy.wait()
        part = pl.ds(s * span, span)

        @pl.loop(0, local // TILE)
        def _(j):
            tile = pl.ds(pl.multiple_of(j * TILE, TILE), TILE)
            for acc, weight in ((gate, vg), (up, vu)):
                term = jnp.dot(x[:, part], weight[part, tile], preferred_element_type=F32)
                acc[:, tile] = term if s == 0 else acc[:, tile] + term

    for s in range(STEPS + 2):
        if s < STEPS:
            relay_over(s)
        if 0 <= s - 1 < STEPS:
            relay_core(s - 1)
        if 0 <= s - 2 < STEPS:
            project(s - 2)

    blocks = []
    for at in range(local // BLOCK):
        tile = pl.ds(at * BLOCK, BLOCK)
        value = gate[:, tile]
        hidden = value / (1.0 + jnp.exp(-value)) * up[:, tile]
        gate[:, tile] = jnp.dot(hidden.astype(BF), table[...], preferred_element_type=F32)
    half = local // 2
    for d in range(n):
        part = pl.ds(d * rows, rows)
        values = gate[part, :]
        turned = walsh([values[:, at * BLOCK:(at + 1) * BLOCK] for at in range(local // BLOCK)])
        values = turned[0] if len(turned) == 1 else jnp.concatenate(turned, axis=1)
        hs[d] = jnp.concatenate([values[:, :half], values[:, half:]], axis=0).astype(BF)

    def exchange(src, dst, at):
        for shift in range(1, n):
            to = lax.rem(me + shift, n)
            send(src.at[to], dst.at[me], a_send.at[at], a_recv.at[at], to)
        dst[me] = src[me]
        settle(dst.at[pl.ds(0, n - 1)], a_recv.at[at])

    exchange(hs, hr, 0)
    factor = 1.0 / math.sqrt(n * local)
    lanes = 128
    for j in range(half // lanes):
        tile = pl.ds(j * lanes, lanes)
        turned = walsh([hr[d, :, tile].astype(F32) for d in range(n)])
        for d in range(n):
            bs[d, :, tile] = (turned[d] * factor).astype(BF)
    exchange(bs, br, 1)

    limit = 127.0 * clip[...]
    for q in range(n // 2):
        pieces = []
        for d in (2 * q, 2 * q + 1):
            values = br[d].astype(F32)
            pieces.append(jnp.concatenate([values[:rows], values[rows:]], axis=1))
        values = jnp.concatenate(pieces, axis=0)
        y[pl.ds(q * both, both), :] = jnp.clip(values, -limit, limit).astype(BF)

    def product(t, half_at, j):
        tile = pl.ds(pl.multiple_of(t * ospan + half_at * opiece + j * TILE, TILE), TILE)
        return jnp.dot(y[...], vd[:, tile], preferred_element_type=F32)

    def down(t):
        down_copies[t].wait()

        @pl.loop(0, opiece // TILE)
        def _(j):
            cs[t, :, pl.ds(pl.multiple_of(j * TILE, TILE), TILE)] = product(t, 1 - c, j).astype(BF)

        send(cs.at[t], cr.at[t], rs_send.at[0], rc_recv.at[t], core_peer)

        @pl.loop(0, opiece // TILE)
        def _(j):
            own[t, :, pl.ds(pl.multiple_of(j * TILE, TILE), TILE)] = product(t, c, j)

    def over_rows(t):
        settle(cr.at[t], rc_recv.at[t])
        for to in range(line):
            part = strip(to, 1 - b)
            ys[t, pl.ds(to * both, both), :] = (own[t, part, :] + cr[t, part, :].astype(F32)).astype(BF)
        send(ys.at[t], yr.at[t], rs_send.at[1], ry_recv.at[t], y_peer)

    def column_sum(t, a_at):
        part = strip(a_at, b)
        landed = yr[t, pl.ds(pl.multiple_of(a_at * both, both), both), :]
        return own[t, part, :] + cr[t, part, :].astype(F32) + landed.astype(F32)

    def over_line(t):
        settle(yr.at[t], ry_recv.at[t])
        for shift in range(1, line):
            zs[t, shift] = column_sum(t, at_line(shift)).astype(BF)
        for shift in range(1, line):
            send(zs.at[t, shift], zr.at[t, shift], rs_send.at[2], rz_recv.at[t], device(at_line(shift)))

    def finish(t):
        settle(zr.at[t, pl.ds(1, line - 1)], rz_recv.at[t])
        values = column_sum(t, a)
        for shift in range(1, line):
            values = values + zr[t, shift].astype(F32)
        fs[t] = jnp.where(first, values[rows:], values[:rows])
        fk[t] = jnp.where(first, values[:rows], values[rows:])
        send(fs.at[t], fr.at[t], rs_send.at[3], rf_recv.at[t], core_peer)

    stages = ((0, down), (LAG[0], over_rows), (LAG[1], over_line), (LAG[2], finish))
    for t in range(OUT_STEPS + LAG[2]):
        for lag, stage in stages:
            if 0 <= t - lag < OUT_STEPS:
                stage(t - lag)
    for t in range(OUT_STEPS):
        settle(fr.at[t], rf_recv.at[t])
        for half_at, sums in ((c, fk), (1 - c, fr)):
            part = pl.ds(pl.multiple_of(t * ospan + half_at * opiece, opiece), opiece)
            out[:, part] = (tok[:, part].astype(F32) + sums[t]).astype(out.dtype)

    settle(tok, pair_sem.at[0])
    settle(x.at[pl.ds(0, total - both), :], ag_send)
    settle(hs.at[pl.ds(0, n - 1)], a_send.at[0])
    settle(bs.at[pl.ds(0, n - 1)], a_send.at[1])
    settle(cs, rs_send.at[0])
    settle(ys, rs_send.at[1])
    settle(zs.at[:, pl.ds(1, line - 1)], rs_send.at[2])
    settle(fs, rs_send.at[3])


def layer(n, tokens, norm_gain, gate_weight, up_weight, down_weight, clip_scale):
    rows, width = tokens.shape
    local = gate_weight.shape[1]
    outs = down_weight.shape[1]
    total, both, line = n * rows, 2 * rows, n // 4
    opiece = outs // OUT_STEPS // 2
    vmem = pl.BlockSpec(memory_space=pltpu.VMEM)
    hbm = pl.BlockSpec(memory_space=pl.ANY)
    dma = pltpu.SemaphoreType.DMA
    swap = pltpu.VMEM((n, both, local // 2), BF)
    return pl.pallas_call(
        functools.partial(kernel, n),
        out_shape=jax.ShapeDtypeStruct((rows, outs), BF),
        in_specs=[vmem, vmem, hbm, hbm, hbm, vmem],
        out_specs=vmem,
        scratch_shapes=[
            pltpu.VMEM((rows, width), BF),
            pltpu.VMEM((total, width), BF),
            pltpu.VMEM((width, local), BF),
            pltpu.VMEM((width, local), BF),
            pltpu.VMEM((local, outs), BF),
            pltpu.VMEM((total, local), F32),
            pltpu.VMEM((total, local), F32),
            pltpu.VMEM((BLOCK, BLOCK), BF),
            swap, swap, swap, swap,
            pltpu.VMEM((total, local), BF),
            pltpu.VMEM((OUT_STEPS, total, opiece), BF),
            pltpu.VMEM((OUT_STEPS, total, opiece), BF),
            pltpu.VMEM((OUT_STEPS, total, opiece), F32),
            pltpu.VMEM((OUT_STEPS, line * both, opiece), BF),
            pltpu.VMEM((OUT_STEPS, line * both, opiece), BF),
            pltpu.VMEM((OUT_STEPS, line, both, opiece), BF),
            pltpu.VMEM((OUT_STEPS, line, both, opiece), BF),
            pltpu.VMEM((OUT_STEPS, rows, opiece), F32),
            pltpu.VMEM((OUT_STEPS, rows, opiece), F32),
            pltpu.VMEM((OUT_STEPS, rows, opiece), F32),
            dma((2, STEPS)), dma((OUT_STEPS,)), dma((2,)), dma(()),
            dma((STEPS, line)), dma((STEPS, line)), dma((STEPS,)),
            dma((2,)), dma((2,)), dma((4,)),
            dma((OUT_STEPS,)), dma((OUT_STEPS,)), dma((OUT_STEPS,)), dma((OUT_STEPS,)),
        ],
        compiler_params=pltpu.CompilerParams(
            collective_id=0, has_side_effects=True, vmem_limit_bytes=67043328),
    )(tokens, norm_gain.reshape(1, -1), gate_weight, up_weight, down_weight, clip_scale.reshape(1, -1))


def solution(mesh):
    in_specs = (
        P(("groups", "hid"), None),
        P(),
        P(None, "hid"),
        P(None, "hid"),
        P("hid", None),
        P("hid"),
    )
    return jax.shard_map(
        functools.partial(layer, mesh.shape["hid"]), mesh=mesh, in_specs=in_specs,
        out_specs=P(("groups", "hid"), None), check_vma=False)
```
